128 devices in a mesh: span: 16 (over y, x), chord: 8 (over z, core).
Axes of the slice: x: 4, y: 4, z: 4, core: 2. Of those that a mesh axis runs over, the one named last changes fastest.
Arguments:
- rhs_fluid: float32 [50, 32768], P(None, ('span', 'chord')), may hold values from -6 to 6
- diag_blocks: float32 [50, 50, 32768], P(None, None, ('span', 'chord')), may hold values from -0.2 to 2.2
- precond_blocks: float32 [50, 50, 32768], P(None, None, ('span', 'chord')), may hold values from -0.04 to 0.49
- face_coupling: float32 [5, 5, 4, 32768], P(None, None, None, ('span', 'chord')), may hold values from -1.75 to 1.75
- neighbors: int32 [4, 32768], P(None, ('span', 'chord')), may hold values from 0 to 1280, as said below
- send_faces: int32 [4, 8192], P(None, ('span', 'chord')), may hold values from 0 to 1023
- flux_weights: float32 [5, 131072], P(None, ('span', 'chord')), may hold values from -3 to 3
- iface_face: int32 [131072], P(('span', 'chord')), may hold values from 0 to 1023
- iface_target: int32 [131072], P(('span', 'chord')), may hold values from 0 to 2047, as said below
- back_weights: float32 [131072], P(('span', 'chord')), may hold values from -6 to 6
- rhs_solid: float32 [262144], P(('span', 'chord')), may hold values from -6 to 6
- solid_blocks: float32 [10, 10, 131072], P(None, None, ('span', 'chord')), may hold values from -0.8 to 3.8
- solid_conn: int32 [10, 131072], P(None, ('span', 'chord')), may hold values from 0 to 2047
- recv_nodes: int32 [6, 262144], P(None, ('span', 'chord')), may hold values from 0 to 2048
- coeffs: float32 [3, 2], replicated, may hold values from 0.3 to 0.9
Outputs:
- flow_adjoint: float32 [50, 32768], P(None, ('span', 'chord'))
- solid_adjoint: float32 [262144], P(('span', 'chord'))
The draws below stay inside these ranges and needn't reach their ends.
Inputs may be any that keep to these rules, and one draw needn't show every extreme that they name: `neighbors`: within each device's block every slot 1024 + j for j below 256 appears exactly once; the value 4 * 256 + 4 * 64 marks a wall face. `iface_target`: within each device's block the values are all the slots of half of the span axis's owners, whose span indices follow one another cyclically, each value once; so every such owner gets exactly 128 faces from that device.
All inputs are finite; a program needn't handle non-finite values.
Results may differ from the reference program's by a relative error of at most 0.0003.
Values sent between devices are 32-bit elements; how exact they have to be, the bound alone decides.
A program may use at most 128 MiB of HBM per device.

```python
import jax
import jax.numpy as jnp
import numpy as np
from jax import lax

FIELDS = 5
NODES = 10
FACE_NODES = 6
NLOC = 50
ITERS = 3
E_DEV = 256
BND = 64
IF_DEV = 1024
SN_DEV = 2048
CAP = 128
ELEMS = 32768
SEND_TOT = 8192
IF_TOT = 131072
SLOTS_TOT = 262144
SE_TOT = 131072
SN_TOT = 262144
N_SPAN = 16
N_CHORD = 8


def draw_diag_blocks(key, part):
    count = FIELDS * NODES
    noise = jax.random.uniform(key, (count, count, ELEMS), jnp.float32, -1.0, 1.0)
    return 2.0 * jnp.eye(count, dtype=jnp.float32)[:, :, None] + 0.8 / count ** 0.5 * noise


def draw_precond_blocks(key, part):
    count = FIELDS * NODES
    noise = jax.random.uniform(key, (count, count, ELEMS), jnp.float32, -1.0, 1.0)
    return 0.45 * jnp.eye(count, dtype=jnp.float32)[:, :, None] + 0.25 / count ** 0.5 * noise


def draw_solid_blocks(key, part):
    noise = jax.random.uniform(key, (NODES, NODES, SE_TOT), jnp.float32, -1.0, 1.0)
    return 3.0 * jnp.eye(NODES, dtype=jnp.float32)[:, :, None] + 0.8 * noise


def draw_neighbors(key, part):
    devices = ELEMS // E_DEV
    columns = 4 * E_DEV
    special = jnp.concatenate([4 * E_DEV + jnp.arange(4 * BND, dtype=jnp.int32), jnp.full((E_DEV // 8,), 4 * E_DEV + 4 * BND, jnp.int32)])

    def one_device(device_key):
        first_key = jax.random.fold_in(device_key, 1)
        second_key = jax.random.fold_in(device_key, 2)
        values = jax.random.randint(first_key, (columns,), 0, columns, jnp.int32)
        order = jax.random.permutation(second_key, columns)
        values = values.at[order[:special.shape[0]]].set(special)
        return values.reshape(4, E_DEV)
    keys = jax.random.split(jax.random.fold_in(key, 7), devices)
    stacked = jax.vmap(one_device)(keys)
    return jnp.transpose(stacked, (1, 0, 2)).reshape(4, ELEMS)


def draw_iface_target(key, part):
    devices = IF_TOT // IF_DEV
    span_count = 2 * IF_DEV // CAP
    chord_count = devices // span_count
    half = span_count // 2
    starts = jax.random.randint(jax.random.fold_in(key, 11), (devices,), 0, half + 1, jnp.int32)
    keys = jax.random.split(jax.random.fold_in(key, 12), devices)

    def one_device(device_index, start, device_key):
        span_index = device_index // chord_count
        owners = (span_index + start + jnp.arange(half, dtype=jnp.int32)) % span_count
        slots = (owners[:, None] * CAP + jnp.arange(CAP, dtype=jnp.int32)[None, :]).reshape(-1)
        order = jax.random.permutation(device_key, IF_DEV)
        return slots[order].astype(jnp.int32)
    stacked = jax.vmap(one_device)(jnp.arange(devices, dtype=jnp.int32), starts, keys)
    return stacked.reshape(-1).astype(jnp.int32)


def with_ends(values, rng, low, largest):
    place = [jax.random.randint(jax.random.fold_in(rng, axis), (), 0, length) for axis, length in enumerate(values.shape)]
    longest = values.shape.index(max(values.shape))
    neighbour = place[:longest] + [(place[longest] + 1) % values.shape[longest]] + place[longest + 1:]
    return values.at[tuple(place)].set(low).at[tuple(neighbour)].set(largest)


def steps_of(rng, dims, shards, least, high):
    loudness = 1.0
    for dim, parts in shards:
        heights = jax.random.uniform(jax.random.fold_in(jax.random.fold_in(rng, 6), dim), (parts,), jnp.float32, least / len(shards), high / len(shards))
        loudness = loudness * jnp.repeat(jnp.exp(heights), dims[dim] // parts).reshape((-1,) + (1,) * (len(dims) - 1 - dim))
    return loudness


def normal_values(own_key, extent, spread, most, shards=(), kind=jnp.bfloat16):
    factor_of = steps_of(own_key, extent, shards, -0.22, 0.18) if shards else 1.0
    values = jax.random.normal(own_key, extent, jnp.float32) * spread * factor_of
    return jnp.minimum(jnp.maximum(values, -most), most).astype(kind)


def setup_inputs(seed: int = 0) -> dict:
    key_list = jax.random.split(jax.random.key(seed), 16)
    return {
        "rhs_fluid": normal_values(key_list[0], (NLOC, ELEMS), 1.0, 6.0, ((1, 128),), jnp.float32),
        "diag_blocks": draw_diag_blocks(jax.random.fold_in(key_list[15], 71), 0),
        "precond_blocks": draw_precond_blocks(jax.random.fold_in(key_list[15], 71), 0),
        "face_coupling": normal_values(key_list[3], (FIELDS, FIELDS, 4, ELEMS), 0.3, 1.75, ((3, 128),), jnp.float32),
        "neighbors": draw_neighbors(jax.random.fold_in(key_list[15], 71), 0),
        "send_faces": with_ends(jax.random.randint(key_list[5], (4, SEND_TOT), 0, 4 * E_DEV), jax.random.fold_in(key_list[5], 1), 0, (4 * E_DEV) - 1).astype(jnp.int32),
        "flux_weights": normal_values(key_list[6], (FIELDS, IF_TOT), 0.5, 3.0, ((1, 128),), jnp.float32),
        "iface_face": with_ends(jax.random.randint(key_list[7], (IF_TOT,), 0, 4 * E_DEV), jax.random.fold_in(key_list[7], 1), 0, (4 * E_DEV) - 1).astype(jnp.int32),
        "iface_target": draw_iface_target(jax.random.fold_in(key_list[15], 71), 0),
        "back_weights": normal_values(key_list[9], (IF_TOT,), 1.0, 6.0, ((0, 128),), jnp.float32),
        "rhs_solid": normal_values(key_list[10], (SN_TOT,), 1.0, 6.0, ((0, 128),), jnp.float32),
        "solid_blocks": draw_solid_blocks(jax.random.fold_in(key_list[15], 71), 0),
        "solid_conn": with_ends(jax.random.randint(key_list[12], (NODES, SE_TOT), 0, SN_DEV), jax.random.fold_in(key_list[12], 1), 0, SN_DEV - 1).astype(jnp.int32),
        "recv_nodes": with_ends(jax.random.randint(key_list[13], (FACE_NODES, SLOTS_TOT), 0, SN_DEV + 1), jax.random.fold_in(key_list[13], 1), 0, SN_DEV).astype(jnp.int32),
        "coeffs": jnp.clip(jax.random.uniform(key_list[14], (ITERS, 2), jnp.float32, 0.3, 0.9), 0.3, 0.9),
    }


face_table = np.array([[1, 2, 3, 7, 8, 9], [0, 2, 3, 5, 6, 9], [0, 1, 3, 4, 6, 8], [0, 1, 2, 4, 5, 7]], dtype=np.int32)
highest = lax.Precision.HIGHEST


def to_blocks(values, devices):
    split = values.reshape(values.shape[:-1] + (devices, values.shape[-1] // devices))
    return jnp.moveaxis(split, -2, 0)


def from_blocks(values):
    moved = jnp.moveaxis(values, 0, -2)
    return moved.reshape(moved.shape[:-2] + (-1,))


def face_traces(adjoint_flow):
    count = adjoint_flow.shape[1]
    shaped = adjoint_flow.reshape(FIELDS, NODES, count)
    pieces = [shaped[:, face_table[face_index], :] for face_index in range(4)]
    return jnp.stack(pieces, axis=2).reshape(FIELDS * FACE_NODES, 4 * count)


def spread_faces(update, count):
    result = jnp.zeros((FIELDS, NODES, count), jnp.float32)
    for face_index in range(4):
        result = result.at[:, face_table[face_index], :].add(update[:, :, face_index, :])
    return result.reshape(FIELDS * NODES, count)


def fluid_local(adjoint_flow, diag_blocks, face_coupling, neighbors, table_local, rims):
    count = adjoint_flow.shape[1]
    table_all = jnp.concatenate([table_local, rims], axis=1)
    picked = jnp.take(table_all, neighbors.reshape(-1), axis=1, mode="fill", fill_value=0.0)
    picked = picked.reshape(FIELDS, FACE_NODES, 4, count)
    update = jnp.einsum("abge,bkge->akge", face_coupling, picked, precision=highest)
    volume = jnp.einsum("ije,je->ie", diag_blocks, adjoint_flow, precision=highest)
    return volume + spread_faces(update, count)


def partial_buffer(table_local, flux_weights, iface_face, iface_target):
    chosen = jnp.take(table_local, iface_face, axis=1).reshape(FIELDS, FACE_NODES, -1)
    partial_flux = jnp.einsum("fi,fki->ki", flux_weights, chosen, precision=highest)
    buffer = jnp.zeros((FACE_NODES, 2 * iface_face.shape[0]), jnp.float32)
    return buffer.at[:, iface_target].set(partial_flux)


def solid_apply(adjoint_solid, solid_blocks, solid_conn, recv_nodes, incoming):
    nodes_count = adjoint_solid.shape[0]
    local_vals = adjoint_solid[solid_conn]
    product = jnp.einsum("abe,be->ae", solid_blocks, local_vals, precision=highest)
    result = jnp.zeros((nodes_count,), jnp.float32).at[solid_conn.reshape(-1)].add(product.reshape(-1))
    added = jnp.zeros((nodes_count + 1,), jnp.float32).at[recv_nodes.reshape(-1)].add(incoming.reshape(-1))
    return result + added[:nodes_count]


def back_buffer(adjoint_solid, recv_nodes):
    padded = jnp.concatenate([adjoint_solid, jnp.zeros((1,), jnp.float32)])
    return padded[recv_nodes]


def add_interface(flow_out, returned, iface_face, iface_target, back_weights):
    count = flow_out.shape[1]
    values = returned[:, iface_target]
    face_index = iface_face // count
    element = iface_face % count
    rows = (FIELDS - 1) * NODES + jnp.asarray(face_table)[face_index]
    flat_index = rows.T * count + element[None, :]
    flat = flow_out.reshape(-1).at[flat_index.reshape(-1)].add((back_weights[None, :] * values).reshape(-1))
    return flat.reshape(flow_out.shape)


def solid_inverse(solid_blocks, solid_conn, nodes_count):
    diagonal_terms = solid_blocks[jnp.arange(NODES), jnp.arange(NODES)]
    assembled = jnp.zeros((nodes_count,), jnp.float32).at[solid_conn.reshape(-1)].add(diagonal_terms.reshape(-1))
    return 1.0 / (1.0 + assembled)


def span_exchange(buffers):
    devices, rows, width = buffers.shape
    grid = buffers.reshape(N_SPAN, N_CHORD, rows, N_SPAN, width // N_SPAN)
    moved = jnp.transpose(grid, (3, 1, 2, 0, 4))
    return moved.reshape(devices, rows, width)


def exchange_rims(outgoing):
    devices, rows, directions, width = outgoing.shape
    grid = outgoing.reshape(N_SPAN, N_CHORD, rows, directions, width)
    slot_zero = jnp.roll(grid[:, :, :, 0, :], 1, axis=0)
    slot_one = jnp.roll(grid[:, :, :, 1, :], -1, axis=0)
    zeros_rim = jnp.zeros_like(grid[:, :1, :, 2, :])
    slot_two = jnp.concatenate([zeros_rim, grid[:, :-1, :, 2, :]], axis=1)
    slot_three = jnp.concatenate([grid[:, 1:, :, 3, :], zeros_rim], axis=1)
    rims = jnp.concatenate([slot_zero, slot_one, slot_two, slot_three], axis=-1)
    return rims.reshape(devices, rows, 4 * width)


def reference(rhs_fluid, diag_blocks, precond_blocks, face_coupling, neighbors, send_faces, flux_weights, iface_face, iface_target, back_weights, rhs_solid, solid_blocks, solid_conn, recv_nodes, coeffs):
    devices = N_SPAN * N_CHORD
    rhs_f = to_blocks(rhs_fluid, devices)
    diag_b = to_blocks(diag_blocks, devices)
    prec_b = to_blocks(precond_blocks, devices)
    coupling_b = to_blocks(face_coupling, devices)
    neigh_b = to_blocks(neighbors, devices)
    send_b = to_blocks(send_faces, devices)
    weights_b = to_blocks(flux_weights, devices)
    iface_b = to_blocks(iface_face, devices)
    target_b = to_blocks(iface_target, devices)
    backw_b = to_blocks(back_weights, devices)
    rhs_s = to_blocks(rhs_solid, devices)
    solid_b = to_blocks(solid_blocks, devices)
    conn_b = to_blocks(solid_conn, devices)
    recv_b = to_blocks(recv_nodes, devices)
    nodes_count = rhs_s.shape[1]
    inverse_diag = jax.vmap(lambda blocks_here, conn_here: solid_inverse(blocks_here, conn_here, nodes_count))(solid_b, conn_b)

    def apply_transposed(adjoint_flow, adjoint_solid):
        table_local = jax.vmap(face_traces)(adjoint_flow)
        outgoing = jax.vmap(lambda table_here, send_here: jnp.take(table_here, send_here.reshape(-1), axis=1).reshape(FIELDS * FACE_NODES, 4, -1))(table_local, send_b)
        rims = exchange_rims(outgoing)
        flow_out = jax.vmap(fluid_local)(adjoint_flow, diag_b, coupling_b, neigh_b, table_local, rims)
        partials = jax.vmap(partial_buffer)(table_local, weights_b, iface_b, target_b)
        incoming = span_exchange(partials)
        solid_out = jax.vmap(solid_apply)(adjoint_solid, solid_b, conn_b, recv_b, incoming)
        returned = span_exchange(jax.vmap(back_buffer)(adjoint_solid, recv_b))
        flow_out = jax.vmap(add_interface)(flow_out, returned, iface_b, target_b, backw_b)
        return flow_out, solid_out

    flow_now = jnp.zeros_like(rhs_f)
    solid_now = jnp.zeros_like(rhs_s)
    flow_prev = jnp.zeros_like(rhs_f)
    solid_prev = jnp.zeros_like(rhs_s)
    for step_index in range(ITERS):
        flow_image, solid_image = apply_transposed(flow_now, solid_now)
        flow_res = rhs_f - flow_image
        solid_res = rhs_s - solid_image
        flow_pre = jnp.einsum("dije,dje->die", prec_b, flow_res, precision=highest)
        solid_pre = inverse_diag * solid_res
        step_size = coeffs[step_index, 0]
        momentum = coeffs[step_index, 1]
        flow_new = flow_now + step_size * flow_pre + momentum * (flow_now - flow_prev)
        solid_new = solid_now + step_size * solid_pre + momentum * (solid_now - solid_prev)
        flow_prev, solid_prev = flow_now, solid_now
        flow_now, solid_now = flow_new, solid_new
    return from_blocks(flow_now), from_blocks(solid_now)
```

```python
import jax
import jax.numpy as jnp
import numpy as np
from jax import lax
from jax.experimental import pallas as pl
from jax.experimental.pallas import tpu as pltpu
from jax.sharding import PartitionSpec as P

FIELDS = 5
NODES = 10
FACE_NODES = 6
ITERS = 3
SPAN = 16
CHORD = 8
MESH = pl.DeviceIdType.MESH
f32 = jnp.float32
bf16 = jnp.bfloat16

face_table = np.array(
    [[1, 2, 3, 7, 8, 9], [0, 2, 3, 5, 6, 9], [0, 1, 3, 4, 6, 8], [0, 1, 2, 4, 5, 7]], dtype=np.int32
)


def spread_matrix():
    table = np.zeros((50, 160), np.float32)
    for g in range(4):
        for k in range(FACE_NODES):
            for a in range(FIELDS):
                table[a * NODES + face_table[g, k], g * 40 + a * 8 + k] = 1.0
    return table


lane_gather = lax.GatherDimensionNumbers(
    offset_dims=(),
    collapsed_slice_dims=(1,),
    start_index_map=(1,),
    operand_batching_dims=(0,),
    start_indices_batching_dims=(0,),
)


def take_lanes(rows, lanes):
    return lax.gather(
        rows,
        lanes[..., None],
        lane_gather,
        (1, 1),
        mode=lax.GatherScatterMode.PROMISE_IN_BOUNDS,
    )


def halves(x):
    high = x.astype(bf16)
    return high, (x - high.astype(f32)).astype(bf16)


def onehot_rows(row, count):
    width = row.shape[1]
    rows = lax.broadcasted_iota(jnp.int32, (count, width), 0)
    return jnp.where(jnp.broadcast_to(row, (count, width)) == rows, 1.0, 0.0).astype(bf16)


def dot_nt(a, b):
    return lax.dot_general(a, b, (((1,), (1,)), ((), ())), preferred_element_type=f32)


def dense_to_row(x):
    return jnp.concatenate([x[r : r + 1] for r in range(x.shape[0])], axis=1)


def gather_faces(u_ref, column):
    shape = column.shape
    lane = column & 127
    right = (column & 128) != 0
    g = column >> 8
    is0, is1, is2, is3, low = g == 0, g == 1, g == 2, g == 3, g < 2
    out = []
    for f in range(FIELDS):
        node = []
        for j in range(NODES):
            r = f * NODES + j
            first = take_lanes(jnp.broadcast_to(u_ref[r : r + 1, 0:128], shape), lane)
            second = take_lanes(jnp.broadcast_to(u_ref[r : r + 1, 128:256], shape), lane)
            node.append(jnp.where(right, second, first))
        out.append(
            [
                jnp.where(is0, node[1], node[0]),
                jnp.where(low, node[2], node[1]),
                jnp.where(is3, node[2], node[3]),
                jnp.where(is0, node[7], jnp.where(is1, node[5], node[4])),
                jnp.where(is0, node[8], jnp.where(is3, node[5], node[6])),
                jnp.where(low, node[9], jnp.where(is2, node[8], node[7])),
            ]
        )
    return out


def gather_nodes(w, index):
    lane, row = index & 127, index >> 7
    picked = jnp.zeros(index.shape, f32)
    for h in range(16):
        source = jnp.broadcast_to(w[h : h + 1], index.shape)
        picked = jnp.where(row == h, take_lanes(source, lane), picked)
    return picked


def block_product(blocks_ref, x, out_ref):
    for i in range(50):
        out_ref[i : i + 1, :] = jnp.sum(blocks_ref[i] * x, axis=0, keepdims=True)


def spread_rows(left_ref, start, values, rows):
    width = values.shape[1]
    step = 512
    for at in range(0, width, step):
        v = jnp.broadcast_to(values[:, at : at + step], (16, step))
        r = jnp.broadcast_to(rows[:, at : at + step], (16, step))
        chosen = jnp.where(r == lax.broadcasted_iota(jnp.int32, (16, step), 0), v, 0.0)
        high, low = halves(chosen)
        left_ref[0:16, start + at : start + at + step] = high
        left_ref[16:32, start + at : start + at + step] = low


def kernel(
    coeffs,
    rhs_fluid_hbm,
    diag_hbm,
    precond_hbm,
    coupling_hbm,
    neighbors_hbm,
    send_faces_hbm,
    flux_hbm,
    iface_face_hbm,
    iface_target_hbm,
    back_weights_hbm,
    rhs_solid_hbm,
    solid_hbm,
    conn_hbm,
    recv_hbm,
    spread_hbm,
    flow_out,
    solid_out,
    rhs_f,
    diag,
    precond,
    coupling,
    neighbors,
    send_faces,
    flux,
    iface_face,
    iface_target,
    back_weights,
    rhs_s,
    solid,
    conn,
    recv,
    spread,
    hot_conn,
    hot_recv,
    hot_face,
    left_conn,
    left_recv,
    permuted,
    left_perm,
    fc,
    local_t,
    vs,
    xs,
    left_face,
    volume,
    flow,
    flow_prev,
    pre,
    wn,
    wp,
    inverse,
    column_perm,
    other_half,
    flux_perm,
    back_perm,
    back_send,
    back_recv,
    part_send,
    part_recv,
    rim_send,
    rim_recv,
    rim_tiles,
    load_sems,
    back_ssem,
    back_rsem,
    part_ssem,
    part_rsem,
    rim_ssem,
    rim_rsem,
):
    s = lax.axis_index("span")
    c = lax.axis_index("chord")
    recv[...] = jnp.full((8, 2048), 2048, jnp.int32)
    loads = {}
    order = (
        ("conn", conn_hbm, conn),
        ("solid", solid_hbm, solid),
        ("recv", recv_hbm, recv.at[0:6]),
        ("rhs_s", rhs_solid_hbm, rhs_s),
        ("rhs_f", rhs_fluid_hbm, rhs_f),
        ("iface_target", iface_target_hbm, iface_target),
        ("iface_face", iface_face_hbm, iface_face),
        ("back_weights", back_weights_hbm, back_weights),
        ("flux", flux_hbm, flux),
        ("send_faces", send_faces_hbm, send_faces),
        ("neighbors", neighbors_hbm, neighbors),
        ("precond", precond_hbm, precond),
        ("coupling", coupling_hbm, coupling),
        ("spread", spread_hbm, spread),
        ("diag", diag_hbm, diag),
    )
    for number, (name, source, target) in enumerate(order):
        loads[name] = pltpu.make_async_copy(source, target, load_sems.at[number])
        loads[name].start()

    barrier = pltpu.get_barrier_semaphore()

    def greet(d, unused):
        pl.semaphore_signal(
            barrier, inc=1, device_id=(lax.rem(s + d, SPAN), c), device_id_type=MESH
        )
        return unused

    lax.fori_loop(1, SPAN, greet, 0)
    up, down = lax.rem(c + 1, CHORD), lax.rem(c + CHORD - 1, CHORD)
    pl.semaphore_signal(barrier, inc=1, device_id=(s, up), device_id_type=MESH)
    pl.semaphore_signal(barrier, inc=1, device_id=(s, down), device_id_type=MESH)

    loads["conn"].wait()
    for a in range(NODES):
        for at in range(0, 1024, 256):
            hot_conn[:, a * 1024 + at : a * 1024 + at + 256] = onehot_rows(
                conn[a : a + 1, at : at + 256] & 127, 128
            )
    loads["recv"].wait()
    for k in range(FACE_NODES):
        for at in range(0, 2048, 256):
            hot_recv[:, k * 2048 + at : k * 2048 + at + 256] = onehot_rows(
                recv[k : k + 1, at : at + 256] & 127, 128
            )

    def scatter_conn():
        both = dot_nt(left_conn[...], hot_conn[...])
        return both[0:16] + both[16:32]

    loads["solid"].wait()
    for a in range(NODES):
        spread_rows(left_conn, a * 1024, solid[a, a : a + 1, :], conn[a : a + 1, :] >> 7)
    inverse[...] = 1.0 / (1.0 + scatter_conn())
    loads["rhs_s"].wait()
    wp[...] = jnp.zeros((16, 128), f32)
    wn[...] = coeffs[0, 0] * (inverse[...] * rhs_s[...])

    for name in ("iface_target", "iface_face", "back_weights", "flux"):
        loads[name].wait()
    target = iface_target[...]
    target_row = dense_to_row((target >> 7) & 7)
    face = iface_face[...]
    weights_all = jnp.concatenate([flux[...], dense_to_row(back_weights[...])], axis=0)
    weights_high = weights_all.astype(bf16).astype(f32)
    pieces = jnp.concatenate(
        [
            weights_high,
            weights_all - weights_high,
            dense_to_row((face >> 7).astype(f32)),
            dense_to_row((face & 127).astype(f32)),
            dense_to_row((target >> 10).astype(f32)),
            jnp.zeros((1, 1024), f32),
        ],
        axis=0,
    )
    for h in range(8):
        left_perm[h * 16 : (h + 1) * 16, :] = jnp.where(
            jnp.broadcast_to(target_row, (16, 1024)) == h, pieces, 0.0
        ).astype(bf16)
    permuted[...] = dot_nt(left_perm[...], onehot_rows(dense_to_row(target & 127), 128))

    def in_slots(x):
        return permuted[pl.ds(x, 8, stride=16), :]

    for f in range(FIELDS):
        flux_perm[f] = in_slots(f) + in_slots(6 + f)
    back_perm[...] = in_slots(5) + in_slots(11)
    face_row = in_slots(12).astype(jnp.int32)
    face_lane = in_slots(13).astype(jnp.int32)
    other_half[...] = in_slots(14)
    hot_face[...] = onehot_rows(dense_to_row(face_lane), 128)
    loads["send_faces"].wait()
    sends = send_faces[...]
    column_perm[0:8, :] = face_row * 128 + face_lane
    column_perm[8:16, :] = jnp.concatenate(
        [
            jnp.concatenate([sends[0:1], sends[1:2]], axis=1),
            jnp.concatenate([sends[2:3], sends[3:4]], axis=1),
            jnp.zeros((6, 128), jnp.int32),
        ],
        axis=0,
    )
    vs[...] = jnp.zeros((320, 128), f32)
    part_send[...] = jnp.zeros((2 * 128, 128), f32)
    rim_send[...] = jnp.zeros((2, 2, 32, 128), f32)

    loads["rhs_f"].wait()
    loads["precond"].wait()
    block_product(precond, rhs_f[...], pre)
    flow[...] = coeffs[0, 0] * pre[...]
    flow_prev[...] = jnp.zeros((50, 256), f32)

    pl.semaphore_wait(barrier, SPAN - 1 + 2)

    for name in ("neighbors", "coupling", "spread", "diag"):
        loads[name].wait()
    for a in range(FIELDS):
        for b in range(FIELDS):
            fc[a * FIELDS + b] = jnp.concatenate(
                [coupling[a, b, :, 0:128], coupling[a, b, :, 128:256]], axis=0
            )

    def sweep(it, unused):
        def back_copy(d):
            peer = lax.rem(s + d, SPAN)
            return pltpu.make_async_remote_copy(
                src_ref=back_send.at[it, peer],
                dst_ref=back_recv.at[it, s],
                send_sem=back_ssem.at[it, d],
                recv_sem=back_rsem.at[it, s],
                device_id=(peer, c),
                device_id_type=MESH,
            )

        def back_arrival(d):
            peer = lax.rem(s + d, SPAN)
            return pltpu.make_async_remote_copy(
                src_ref=back_send.at[it, peer],
                dst_ref=back_recv.at[it, peer],
                send_sem=back_ssem.at[it, d],
                recv_sem=back_rsem.at[it, peer],
                device_id=(peer, c),
                device_id_type=MESH,
            )

        def part_rows(owner):
            return part_send.at[pl.ds(pl.multiple_of(it * 128 + owner * 8, 8), 8), :]

        def part_copy(d):
            peer = lax.rem(s + d, SPAN)
            return pltpu.make_async_remote_copy(
                src_ref=part_rows(peer),
                dst_ref=part_recv.at[it, s],
                send_sem=part_ssem.at[it, d],
                recv_sem=part_rsem.at[it, s],
                device_id=(peer, c),
                device_id_type=MESH,
            )

        def part_arrival(d):
            peer = lax.rem(s + d, SPAN)
            return pltpu.make_async_remote_copy(
                src_ref=part_rows(peer),
                dst_ref=part_recv.at[it, peer],
                send_sem=part_ssem.at[it, d],
                recv_sem=part_rsem.at[it, peer],
                device_id=(peer, c),
                device_id_type=MESH,
            )

        def rim_copy(slot):
            there = (
                (lax.rem(s + 1, SPAN), c),
                (lax.rem(s + SPAN - 1, SPAN), c),
                (s, up),
                (s, down),
            )[slot]
            return pltpu.make_async_remote_copy(
                src_ref=rim_send.at[it, slot // 2],
                dst_ref=rim_recv.at[it, slot],
                send_sem=rim_ssem.at[it, slot],
                recv_sem=rim_rsem.at[it, slot],
                device_id=there,
                device_id_type=MESH,
            )

        def each_peer(act):
            def body(d, unused):
                act(d)
                return unused

            lax.fori_loop(1, SPAN, body, 0)

        w = wn[...]
        for src in range(SPAN):
            back_send[it, src] = gather_nodes(w, recv[:, src * 128 : (src + 1) * 128])
        each_peer(lambda d: back_copy(d).start())
        back_recv[it, s] = back_send[it, s]

        picked = gather_faces(flow, column_perm[...])
        for f in range(FIELDS):
            for k in range(FACE_NODES):
                r = f * FACE_NODES + k
                rim_send[it, 0, r : r + 1, :] = picked[f][k][8:9]
                rim_send[it, 1, r : r + 1, :] = picked[f][k][9:10]
        for slot in range(4):
            rim_copy(slot).start()
        second = other_half[...] != 0.0
        for k in range(FACE_NODES):
            q = flux_perm[0] * picked[0][k][0:8]
            for f in range(1, FIELDS):
                q = q + flux_perm[f] * picked[f][k][0:8]
            both = jnp.concatenate([jnp.where(second, 0.0, q), jnp.where(second, q, 0.0)], axis=0)
            part_send[pl.ds(it * 128 + k, SPAN, stride=8), :] = both
        each_peer(lambda d: part_copy(d).start())
        part_recv[it, s] = part_send[pl.ds(pl.multiple_of(it * 128 + s * 8, 8), 8), :]

        here = neighbors[...]
        column = jnp.concatenate([here[:, 0:128], here[:, 128:256]], axis=0)
        picked = gather_faces(flow, column)
        for f in range(FIELDS):
            for k in range(FACE_NODES):
                local_t[f * FACE_NODES + k] = picked[f][k]
        block_product(diag, flow[...], volume)

        low_rows = conn[8:10, :]
        index = jnp.concatenate(
            [conn[0:8, t * 128 : (t + 1) * 128] for t in range(8)]
            + [low_rows[:, t * 128 : (t + 1) * 128] for t in range(8)],
            axis=0,
        )
        vals = gather_nodes(w, index)
        at_elements = jnp.concatenate(
            [
                jnp.concatenate([vals[t * 8 : (t + 1) * 8] for t in range(8)], axis=1),
                jnp.concatenate([vals[64 + t * 2 : 66 + t * 2] for t in range(8)], axis=1),
            ],
            axis=0,
        )
        for a in range(NODES):
            product = jnp.sum(solid[a] * at_elements, axis=0, keepdims=True)
            spread_rows(left_conn, a * 1024, product, conn[a : a + 1, :] >> 7)
        solid_image = scatter_conn()

        for slot in range(4):
            rim_copy(slot).wait()
        first_half = lax.broadcasted_iota(jnp.int32, (32, 128), 1) < 64
        rim_tiles[0] = jnp.where(first_half, rim_recv[it, 0], rim_recv[it, 1])
        rim_tiles[1] = jnp.where(
            first_half,
            jnp.where(c > 0, rim_recv[it, 2], 0.0),
            jnp.where(c < CHORD - 1, rim_recv[it, 3], 0.0),
        )
        lane, tile = column & 127, column >> 7
        inside, span_rim, chord_rim = tile < 8, tile == 8, tile == 9
        traces = []
        for r in range(FIELDS * FACE_NODES):
            one = take_lanes(jnp.broadcast_to(rim_tiles[0, r : r + 1, :], (8, 128)), lane)
            two = take_lanes(jnp.broadcast_to(rim_tiles[1, r : r + 1, :], (8, 128)), lane)
            traces.append(
                jnp.where(
                    inside,
                    local_t[r],
                    jnp.where(span_rim, one, jnp.where(chord_rim, two, 0.0)),
                )
            )
        for a in range(FIELDS):
            for k in range(FACE_NODES):
                v = fc[a * FIELDS] * traces[k]
                for b in range(1, FIELDS):
                    v = v + fc[a * FIELDS + b] * traces[b * FACE_NODES + k]
                at = (a * 8 + k) * 8
                vs[at : at + 8, :] = v

        each_peer(lambda d: back_arrival(d).wait())
        back = []
        for h in range(8):
            chosen = jnp.where(
                jnp.broadcast_to(second[h : h + 1], (8, 128)),
                back_recv[it, h + 8],
                back_recv[it, h],
            )
            back.append(chosen * back_perm[h : h + 1, :])
        back = jnp.concatenate(back, axis=1)
        face_rows = jnp.broadcast_to(dense_to_row(column_perm[0:8, :] >> 7), (8, 1024))
        for tile_number in range(8):
            left_face[tile_number * 8 : (tile_number + 1) * 8, :] = jnp.where(
                face_rows == tile_number, back, 0.0
            )
        high, low = halves(left_face[...])
        on_faces = dot_nt(high, hot_face[...]) + dot_nt(low, hot_face[...])
        for half in range(2):
            for g in range(4):
                lanes = slice(half * 128, half * 128 + 128)
                block = vs[pl.ds(half * 4 + g, 40, stride=8), :]
                t = g * 2 + half
                xs[g * 40 : g * 40 + 32, lanes] = block[0:32]
                xs[g * 40 + 32 : g * 40 + 40, lanes] = block[32:40] + on_faces[t * 8 : t * 8 + 8]
        high, low = halves(xs[...])
        matrix = spread[...]
        faces = jnp.dot(matrix, high, preferred_element_type=f32) + jnp.dot(
            matrix, low, preferred_element_type=f32
        )
        volume[...] = rhs_f[...] - (volume[...] + faces)
        block_product(precond, volume[...], pre)
        now = flow[...]
        new = now + coeffs[it + 1, 0] * pre[...] + coeffs[it + 1, 1] * (now - flow_prev[...])
        flow_prev[...] = now
        flow[...] = new

        each_peer(lambda d: part_arrival(d).wait())
        incoming = jnp.concatenate([part_recv[it, src] for src in range(SPAN)], axis=1)
        for k in range(FACE_NODES):
            spread_rows(left_recv, k * 2048, incoming[k : k + 1], recv[k : k + 1, :] >> 7)
        both = dot_nt(left_recv[...], hot_recv[...])
        residual = rhs_s[...] - (solid_image + (both[0:16] + both[16:32]))
        w_new = (
            w
            + coeffs[it + 1, 0] * (inverse[...] * residual)
            + coeffs[it + 1, 1] * (w - wp[...])
        )
        wp[...] = w
        wn[...] = w_new
        return unused

    lax.fori_loop(0, ITERS - 1, sweep, 0)
    flow_out[...] = flow[...]
    solid_out[...] = wn[...]


def per_device(
    rhs_fluid,
    diag_blocks,
    precond_blocks,
    face_coupling,
    neighbors,
    send_faces,
    flux_weights,
    iface_face,
    iface_target,
    back_weights,
    rhs_solid,
    solid_blocks,
    solid_conn,
    recv_nodes,
    coeffs,
):
    i32 = jnp.int32
    hbm = pl.BlockSpec(memory_space=pl.ANY)
    vmem = pl.BlockSpec(memory_space=pltpu.VMEM)
    dma = pltpu.SemaphoreType.DMA
    V = pltpu.VMEM
    flow, solid = pl.pallas_call(
        kernel,
        name="coupled_sweeps",
        out_shape=(
            jax.ShapeDtypeStruct((50, 256), f32),
            jax.ShapeDtypeStruct((16, 128), f32),
        ),
        in_specs=[pl.BlockSpec(memory_space=pltpu.SMEM)] + [hbm] * 15,
        out_specs=(vmem, vmem),
        scratch_shapes=[
            V((50, 256), f32),
            V((50, 50, 256), f32),
            V((50, 50, 256), f32),
            V((5, 5, 4, 256), f32),
            V((4, 256), i32),
            V((4, 64), i32),
            V((5, 1024), f32),
            V((8, 128), i32),
            V((8, 128), i32),
            V((8, 128), f32),
            V((16, 128), f32),
            V((10, 10, 1024), f32),
            V((10, 1024), i32),
            V((8, 2048), i32),
            V((50, 160), bf16),
            V((128, 10 * 1024), bf16),
            V((128, 6 * 2048), bf16),
            V((128, 1024), bf16),
            V((32, 10 * 1024), bf16),
            V((32, 6 * 2048), bf16),
            V((128, 128), f32),
            V((128, 1024), bf16),
            V((25, 8, 128), f32),
            V((30, 8, 128), f32),
            V((320, 128), f32),
            V((160, 256), f32),
            V((64, 1024), f32),
            V((50, 256), f32),
            V((50, 256), f32),
            V((50, 256), f32),
            V((50, 256), f32),
            V((16, 128), f32),
            V((16, 128), f32),
            V((16, 128), f32),
            V((16, 128), i32),
            V((8, 128), f32),
            V((5, 8, 128), f32),
            V((8, 128), f32),
            V((2, SPAN, 8, 128), f32),
            V((2, SPAN, 8, 128), f32),
            V((2 * 128, 128), f32),
            V((2, SPAN, 8, 128), f32),
            V((2, 2, 32, 128), f32),
            V((2, 4, 32, 128), f32),
            V((2, 32, 128), f32),
            dma((15,)),
            dma((2, SPAN)),
            dma((2, SPAN)),
            dma((2, SPAN)),
            dma((2, SPAN)),
            dma((2, 4)),
            dma((2, 4)),
        ],
        compiler_params=pltpu.CompilerParams(
            collective_id=0, has_side_effects=True, vmem_limit_bytes=48 << 20
        ),
    )(
        coeffs,
        rhs_fluid,
        diag_blocks,
        precond_blocks,
        face_coupling,
        neighbors,
        send_faces,
        flux_weights,
        iface_face.reshape(8, 128),
        iface_target.reshape(8, 128),
        back_weights.reshape(8, 128),
        rhs_solid.reshape(16, 128),
        solid_blocks,
        solid_conn,
        recv_nodes,
        jnp.asarray(spread_matrix(), bf16),
    )
    return flow, solid.reshape(2048)


def solution(mesh):
    in_specs = (
        P(None, ("span", "chord")),
        P(None, None, ("span", "chord")),
        P(None, None, ("span", "chord")),
        P(None, None, None, ("span", "chord")),
        P(None, ("span", "chord")),
        P(None, ("span", "chord")),
        P(None, ("span", "chord")),
        P(("span", "chord")),
        P(("span", "chord")),
        P(("span", "chord")),
        P(("span", "chord")),
        P(None, None, ("span", "chord")),
        P(None, ("span", "chord")),
        P(None, ("span", "chord")),
        P(),
    )
    out_specs = (P(None, ("span", "chord")), P(("span", "chord")))
    return jax.shard_map(
        per_device, mesh=mesh, in_specs=in_specs, out_specs=out_specs, check_vma=False
    )
```
